32 devices in a mesh: grp: 2 (over y), row: 4 (over z), col: 4 (over x, core).
Axes of the slice: x: 2, y: 2, z: 4, core: 2. Of those that a mesh axis runs over, the one named last changes fastest.
Arguments:
- activations: bfloat16 [1024, 6144], P(('grp', 'col'), 'row'), parts along dimension 0, may hold values from -6 to 6
- out_grads: bfloat16 [1024, 18432], P(('grp', 'row'), 'col'), parts along dimension 0, may hold values from -0.1796875 to 0.1796875
- matrix: bfloat16 [12288, 18432], P(('grp', 'row'), 'col'), parts along dimension 0, may hold values from -30 to 30
- left: bfloat16 [12288, 256], P(('grp', 'row')), parts along dimension 0, may hold values from -4 to 4
- right: bfloat16 [36864, 256], P(('grp', 'col')), parts along dimension 0, may hold values from -4 to 4
Outputs:
- left_new: bfloat16 [12288, 256], P(('grp', 'row')), parts along dimension 0
- right_new: bfloat16 [36864, 256], P(('grp', 'col')), parts along dimension 0
- residual: bfloat16 [12288, 18432], P(('grp', 'row'), 'col'), parts along dimension 0
The draws below stay inside these ranges and needn't reach their ends.
There are 2 independent parts, one for each index of `grp`. The reference program is written for one: setup_inputs(seed, part) draws one part's arguments, and reference() takes and returns one part's arrays. A program takes and returns all parts, laid end to end along the dimension named above; each array names one. Nothing has to cross between parts.
All inputs are finite; a program needn't handle non-finite values.
Results may differ from the reference program's by a relative error of at most 0.0034.
Values may be sent and summed in bfloat16 or wider, within the bound.
A program may use at most 192 MiB of HBM per device.

```python
import math
import jax
import jax.numpy as jnp
from jax import lax

M = 6144
N = 18432
RANK = 256
TOKENS = 512


def factor_base(key, shape):
    return jnp.clip(jax.random.normal(key, shape, jnp.float32), -6.0, 6.0)


def factor_parts(key):
    keys = jax.random.split(jax.random.fold_in(key, 53), 6)
    row_scale = jnp.exp(jax.random.uniform(keys[0], (M, 1), jnp.float32, 0.0, math.log(10.0)))
    column_pos = jnp.arange(N, dtype=jnp.float32)[:, None] / N
    col_scale = jnp.exp(column_pos * math.log(3.0) + jax.random.uniform(keys[1], (N, 1), jnp.float32, -0.5, 0.5))
    left_spread = 0.8 / math.sqrt(RANK)
    right_spread = 0.1
    left_full = jnp.clip(row_scale * left_spread * factor_base(keys[2], (M, RANK)), -4.0, 4.0)
    left_target = left_full + row_scale * left_spread * factor_base(keys[3], (M, RANK))
    right_full = jnp.clip(col_scale * right_spread * factor_base(keys[4], (N, RANK)), -4.0, 4.0)
    right_target = right_full + col_scale * right_spread * factor_base(keys[5], (N, RANK))
    return (left_full, right_full, left_target, right_target, row_scale, col_scale)


def draw_left(key, part):
    return factor_parts(key)[0].astype(jnp.bfloat16)


def draw_right(key, part):
    return factor_parts(key)[1].astype(jnp.bfloat16)


def draw_matrix(key, part):
    left_full, right_full, left_target, right_target, row_scale, col_scale = factor_parts(key)
    low_part = jnp.dot(left_target, right_target.T)
    noise_key = jax.random.fold_in(key, 97)
    noise_base = jnp.clip(jax.random.normal(noise_key, (M, N), jnp.float32), -6.0, 6.0)
    noise = 0.03 * noise_base * row_scale * col_scale.T
    return jnp.clip(low_part + noise, -30.0, 30.0).astype(jnp.bfloat16)


def block_scale(stream_key, extent, shards, least, largest):
    def one(axis_at, parts):
        heights = jax.random.uniform(jax.random.fold_in(jax.random.fold_in(stream_key, 6), axis_at), (parts,), jnp.float32, least / len(shards), largest / len(shards))
        return jnp.repeat(jnp.exp(heights), extent[axis_at] // parts).reshape((-1,) + (1,) * (len(extent) - axis_at - 1))

    level = one(*shards[0])
    for cut in shards[1:]:
        level = level * one(*cut)
    return level


def normal_values(rng, dims, deviation, limit, cuts=(), held_as=jnp.bfloat16):
    drawn = jax.random.normal(rng, dims, jnp.float32) * deviation
    if len(cuts) > 0:
        drawn = block_scale(rng, dims, cuts, -0.22, 0.18) * drawn
    return jnp.clip(drawn, min=-limit, max=limit).astype(held_as)


def setup_inputs(seed: int = 0, part: int = 0) -> dict:
    streams_of = jax.random.split(jax.random.key(seed), 6)
    part_splits = jax.random.split(jax.random.fold_in(streams_of[5], part), 6)
    return {
        "activations": normal_values(part_splits[0], (TOKENS, M), 1.0, 6.0, ((0, 4), (1, 4))),
        "out_grads": normal_values(part_splits[1], (TOKENS, N), 0.03, 0.1796875, ((0, 4), (1, 4))),
        "matrix": draw_matrix(jax.random.fold_in(jax.random.fold_in(streams_of[5], part), 71), part),
        "left": draw_left(jax.random.fold_in(jax.random.fold_in(streams_of[5], part), 71), part),
        "right": draw_right(jax.random.fold_in(jax.random.fold_in(streams_of[5], part), 71), part),
    }


epsilon = 1e-6


def contract_rank(first, second):
    return lax.dot_general(first, second, (((1,), (1,)), ((), ())), preferred_element_type=jnp.float32)


def reference(activations, out_grads, matrix, left, right):
    gradient = lax.dot_general(activations, out_grads, (((0,), (0,)), ((), ())), preferred_element_type=jnp.float32)
    wfloat = matrix.astype(jnp.float32)
    fisher = 1.0 + (wfloat * gradient) ** 2
    early_residual = wfloat - contract_rank(left, right)
    weighted_early = (fisher * early_residual).astype(jnp.bfloat16)
    left_descent = jnp.dot(weighted_early, right, preferred_element_type=jnp.float32)
    left_image = contract_rank(left_descent.astype(jnp.bfloat16), right)
    left_step = jnp.sum(left_descent * left_descent) / (jnp.sum(fisher * left_image * left_image) + epsilon)
    left_new = (left.astype(jnp.float32) + left_step * left_descent).astype(jnp.bfloat16)
    later_residual = early_residual - left_step * left_image
    weighted_later = (fisher * later_residual).astype(jnp.bfloat16)
    right_descent = lax.dot_general(weighted_later, left_new, (((0,), (0,)), ((), ())), preferred_element_type=jnp.float32)
    right_image = contract_rank(left_new, right_descent.astype(jnp.bfloat16))
    right_step = jnp.sum(right_descent * right_descent) / (jnp.sum(fisher * right_image * right_image) + epsilon)
    right_new = (right.astype(jnp.float32) + right_step * right_descent).astype(jnp.bfloat16)
    residual = (later_residual - right_step * right_image).astype(jnp.bfloat16)
    return left_new, right_new, residual
```

```python
import functools

import jax
import jax.numpy as jnp
from jax import lax
from jax.experimental import pallas as pl
from jax.experimental.pallas import tpu as pltpu
from jax.sharding import PartitionSpec as P

epsilon = 1e-06
f32 = jnp.float32
bf16 = jnp.bfloat16
MESH = pl.DeviceIdType.MESH


def pick(extent, cap, unit):
    best = unit
    for size in range(unit, cap + 1, unit):
        if extent % size == 0:
            best = size
    return best


def mm(a, b):
    return jnp.dot(a, b, preferred_element_type=f32)


def mm_nt(a, b):
    return lax.dot_general(a, b, (((1,), (1,)), ((), ())), preferred_element_type=f32)


def main_kernel(
    nr, nc, nch, chunk, tile,
    act_hbm, og_hbm, w_hbm, l_ref, r_ref,
    ln_ref, ldr_ref, t_hbm, s_ref,
    fisher, wbuf, ogb, actb, actt, lpart, lsend, lr1, lh, lr2, ld4, lnt,
    part, inb, exb, tot, rp, acc, sc, sr,
    wsem, ogsem, asem, act_s, act_r, up_s, up_r, dn_s, dn_r,
    l1, l2s, l2r, l3s, l3r, l4, cs, cr, rs, rr,
    in_s, in_r, ex_s, ex_r, out_s, out_r, tsem,
):
    g = lax.axis_index("grp")
    r = lax.axis_index("row")
    c = lax.axis_index("col")
    nx = nc // 2
    rows = l_ref.shape[0]
    q = rows // nc
    nt = rows // tile
    lanes = pick(rows, 256, 128)

    def at(row, col):
        return (g, row, col)

    def remote(src, dst, ss, rs_, dev):
        return pltpu.make_async_remote_copy(
            src_ref=src, dst_ref=dst, send_sem=ss, recv_sem=rs_, device_id=dev, device_id_type=MESH
        )

    def w_copy(k, slot):
        cols = pl.ds(pl.multiple_of(k * chunk, 128), chunk)
        return pltpu.make_async_copy(w_hbm.at[:, cols], wbuf.at[slot], wsem.at[slot])

    def og_local(k):
        cols = pl.ds(pl.multiple_of(k * chunk, 128), chunk)
        return pltpu.make_async_copy(og_hbm.at[:, cols], ogb.at[k, r], ogsem.at[k])

    act_local = pltpu.make_async_copy(act_hbm, actb.at[c], asem)
    act_local.start()

    def start_og(k, carry):
        og_local(k).start()
        return carry

    lax.fori_loop(0, nch, start_og, 0)
    w_copy(0, 0).start()

    bar = pltpu.get_barrier_semaphore()
    for d in range(1, nr):
        pl.semaphore_signal(bar, inc=1, device_id=at(lax.rem(r + d, nr), c), device_id_type=MESH)
    for d in range(1, nc):
        pl.semaphore_signal(bar, inc=1, device_id=at(r, lax.rem(c + d, nc)), device_id_type=MESH)
    pl.semaphore_wait(bar, nr + nc - 2)

    act_local.wait()

    def act_copy(d):
        return remote(actb.at[c], actb.at[c], act_s.at[d - 1], act_r.at[d - 1], at(r, lax.rem(c + d, nc)))

    for d in range(1, nc):
        act_copy(d).start()

    def up_copy(k, s):
        blk = jnp.maximum(r - s, 0)
        return remote(ogb.at[k, blk], ogb.at[k, blk], up_s.at[k, s], up_r.at[k, s], at(jnp.minimum(r + 1, nr - 1), c))

    def dn_copy(k, s):
        blk = jnp.minimum(r + s, nr - 1)
        return remote(ogb.at[k, blk], ogb.at[k, blk], dn_s.at[k, s], dn_r.at[k, s], at(jnp.maximum(r - 1, 0), c))

    def up_sends(s):
        return jnp.logical_and(r - s >= 0, r + 1 < nr)

    def dn_sends(s):
        return jnp.logical_and(r + s < nr, r >= 1)

    def up_wait(k, s):
        blk = jnp.maximum(r - 1 - s, 0)
        remote(ogb.at[k, blk], ogb.at[k, blk], up_s.at[k, s], up_r.at[k, s], at(jnp.minimum(r + 1, nr - 1), c)).wait_recv()

    def dn_wait(k, s):
        blk = jnp.minimum(r + 1 + s, nr - 1)
        remote(ogb.at[k, blk], ogb.at[k, blk], dn_s.at[k, s], dn_r.at[k, s], at(jnp.maximum(r - 1, 0), c)).wait_recv()

    lpart[...] = jnp.zeros_like(lpart)
    acc[...] = jnp.zeros_like(acc)

    def rows_at(i):
        return pl.ds(pl.multiple_of(i * tile, tile), tile)

    def cols_at(k):
        return pl.ds(pl.multiple_of(k * chunk, chunk), chunk)

    def pass_a(k):
        slot = lax.rem(k, 2)
        w_copy(lax.rem(k + 1, nch), lax.rem(k + 1, 2)).start()
        w_copy(k, slot).wait()

        def step(i, carry):
            rw = rows_at(i)
            og = ogb[k].reshape(-1, chunk)
            grad = mm(actt[rw, :], og)
            w = wbuf[slot, rw, :].astype(f32)
            rj = r_ref[cols_at(k), :]
            wg = w * grad
            fish = 1.0 + wg * wg
            fisher[k, rw, :] = fish
            early = w - mm_nt(l_ref[rw, :], rj)
            lpart[rw, :] += mm((fish * early).astype(bf16), rj)
            return carry

        lax.fori_loop(0, nt, step, 0)

    def gather_step(j, carry):
        @pl.when(j < nch)
        def _():
            og_local(j).wait()

            @pl.when(up_sends(0))
            def _():
                up_copy(j, 0).start()

            @pl.when(dn_sends(0))
            def _():
                dn_copy(j, 0).start()

        for s in range(1, nr):
            k = j - s

            @pl.when(jnp.logical_and(k >= 0, k < nch))
            def _():
                @pl.when(r - s >= 0)
                def _():
                    up_wait(k, s - 1)

                @pl.when(up_sends(s))
                def _():
                    up_copy(k, s).start()

                @pl.when(r + s < nr)
                def _():
                    dn_wait(k, s - 1)

                @pl.when(dn_sends(s))
                def _():
                    dn_copy(k, s).start()

        @pl.when(j == nr - 1)
        def _():
            for d in range(1, nc):
                src = lax.rem(c + nc - d, nc)
                remote(actb.at[src], actb.at[src], act_s.at[d - 1], act_r.at[d - 1], at(r, src)).wait_recv()

            def turn(i, carry):
                rw = pl.ds(pl.multiple_of(i * lanes, lanes), lanes)
                block = actb[:, :, rw].reshape(-1, lanes)
                actt[rw, :] = block.astype(f32).T.astype(bf16)
                return carry

            lax.fori_loop(0, rows // lanes, turn, 0)

        @pl.when(j >= nr - 1)
        def _():
            pass_a(j - (nr - 1))

        return carry

    lax.fori_loop(0, nch + nr - 1, gather_step, 0)

    def drain_og(k, carry):
        for s in range(nr - 1):
            @pl.when(up_sends(s))
            def _():
                up_copy(k, s).wait_send()

            @pl.when(dn_sends(s))
            def _():
                dn_copy(k, s).wait_send()
        return carry

    par = lax.rem(c, 2)
    x = c // 2
    mate = at(r, c + 1 - 2 * par)
    for k in range(nc):
        lsend[k % 2, k // 2] = lpart[k * q:(k + 1) * q, :].astype(bf16)
    one = remote(lsend.at[1 - par], lr1, l1.at[0], l1.at[1], mate)
    one.start()
    one.wait()

    def own_rows(xx):
        return lpart[pl.ds(pl.multiple_of((2 * xx + par) * q, 8), q), :] + lr1[xx].astype(f32)

    for d in range(1, nx):
        xx = lax.rem(x + d, nx)
        lh[d - 1] = own_rows(xx).astype(bf16)
        remote(lh.at[d - 1], lr2.at[d - 1], l2s.at[d - 1], l2r.at[d - 1], at(r, 2 * xx + par)).start()
    desc = own_rows(x)
    for d in range(1, nx):
        xx = lax.rem(x + d, nx)
        remote(lh.at[d - 1], lr2.at[d - 1], l2s.at[d - 1], l2r.at[d - 1], at(r, 2 * xx + par)).wait()
        desc = desc + lr2[d - 1].astype(f32)
    norm = jnp.sum(jnp.sum(desc * desc, axis=0, keepdims=True), axis=1, keepdims=True)
    ld4[par, x] = desc.astype(bf16)
    for d in range(1, nx):
        xx = lax.rem(x + d, nx)
        remote(ld4.at[par, x], ld4.at[par, x], l3s.at[d - 1], l3r.at[d - 1], at(r, 2 * xx + par)).start()
    for d in range(1, nx):
        xx = lax.rem(x + nx - d, nx)
        got = remote(ld4.at[par, xx], ld4.at[par, xx], l3s.at[d - 1], l3r.at[d - 1], at(r, 2 * xx + par))
        got.wait_recv()
    remote(ld4.at[par], ld4.at[par], l4.at[0], l4.at[1], mate).start()
    remote(ld4.at[1 - par], ld4.at[1 - par], l4.at[0], l4.at[1], mate).wait_recv()
    for k in range(nc):
        lpart[k * q:(k + 1) * q, :] = ld4[k % 2, k // 2].astype(f32)

    def cast_left(i, carry):
        ldr_ref[rows_at(i), :] = lpart[rows_at(i), :].astype(bf16)
        return carry

    lax.fori_loop(0, nt, cast_left, 0)

    def curve_tile(fish, image):
        weighted = fish * image * image
        acc[...] += jnp.sum(weighted.reshape(tile // 8, 8, chunk), axis=0)

    def pass_b(k, carry):
        def step(i, inner):
            rw = rows_at(i)
            curve_tile(fisher[k, rw, :], mm_nt(ldr_ref[rw, :], r_ref[cols_at(k), :]))
            return inner

        return lax.fori_loop(0, nt, step, carry)

    lax.fori_loop(0, nch, pass_b, 0)

    def total(t, norm_part):
        curve = jnp.sum(jnp.sum(acc[...], axis=0, keepdims=True), axis=1, keepdims=True)
        top = lax.broadcasted_iota(jnp.int32, (8, 128), 0) == 0
        sc[t, c] = jnp.where(top, jnp.broadcast_to(curve, (8, 128)), jnp.broadcast_to(norm_part, (8, 128)))
        for d in range(1, nc):
            remote(sc.at[t, c], sc.at[t, c], cs.at[t, d - 1], cr.at[t, d - 1], at(r, lax.rem(c + d, nc))).start()
        for d in range(1, nc):
            src = lax.rem(c + nc - d, nc)
            remote(sc.at[t, src], sc.at[t, src], cs.at[t, d - 1], cr.at[t, d - 1], at(r, src)).wait_recv()
        sr[t, r] = jnp.sum(sc[t], axis=0)
        for d in range(1, nr):
            remote(sr.at[t, r], sr.at[t, r], rs.at[t, d - 1], rr.at[t, d - 1], at(lax.rem(r + d, nr), c)).start()
        for d in range(1, nr):
            src = lax.rem(r + nr - d, nr)
            remote(sr.at[t, src], sr.at[t, src], rs.at[t, d - 1], rr.at[t, d - 1], at(src, c)).wait_recv()
        both = jnp.sum(sr[t], axis=0)
        return both[1:2, :] / (both[0:1, :] + epsilon)

    s_ref[0:1, :] = total(0, norm)

    def make_left(i, carry):
        rw = rows_at(i)
        new = (l_ref[rw, :].astype(f32) + s_ref[0:1, 0:1] * lpart[rw, :]).astype(bf16)
        ln_ref[rw, :] = new
        lnt[i] = new.astype(f32).T.astype(bf16)
        return carry

    lax.fori_loop(0, nt, make_left, 0)
    acc[...] = jnp.zeros_like(acc)

    half = nr // 2
    lower = r < half
    inn = at(jnp.where(lower, r + 1, r - 1), c)
    outn = at(jnp.where(lower, jnp.maximum(r - 1, 0), jnp.minimum(r + 1, nr - 1)), c)
    mid = jnp.logical_or(r == half - 1, r == half)
    edge = jnp.logical_or(r == 0, r == nr - 1)
    not_mid = jnp.logical_not(mid)
    not_edge = jnp.logical_not(edge)

    def in_copy(k):
        return remote(part.at[k], inb.at[k], in_s.at[k], in_r.at[k], inn)

    def ex_copy(k):
        return remote(part.at[k], exb.at[k], ex_s.at[k], ex_r.at[k], inn)

    def out_copy(k):
        return remote(tot.at[k], tot.at[k], out_s.at[k], out_r.at[k], outn)

    def pass_c(k):
        slot = lax.rem(k + nch, 2)

        @pl.when(k + 1 < nch)
        def _():
            w_copy(k + 1, lax.rem(k + 1 + nch, 2)).start()

        w_copy(k, slot).wait()
        rp[...] = jnp.zeros_like(rp)

        def step(i, carry):
            rw = rows_at(i)
            rj = r_ref[cols_at(k), :]
            later = wbuf[slot, rw, :].astype(f32) - mm_nt(l_ref[rw, :], rj)
            later = later - s_ref[0:1, 0:1] * mm_nt(ldr_ref[rw, :], rj)
            rp[...] += mm(lnt[i], (fisher[k, rw, :] * later).astype(bf16))
            return carry

        lax.fori_loop(0, nt, step, 0)
        part[k] = rp[...].astype(bf16)

    def pass_d(k):
        def step(i, carry):
            rw = rows_at(i)
            curve_tile(fisher[k, rw, :], mm(ln_ref[rw, :], tot[k]))
            return carry

        lax.fori_loop(0, nt, step, 0)

    lag = 2

    def right_step(j, carry):
        @pl.when(j < nch)
        def _():
            pass_c(j)

            @pl.when(jnp.logical_and(edge, not_mid))
            def _():
                in_copy(j).start()

        a = j - lag

        @pl.when(jnp.logical_and(a >= 0, a < nch))
        def _():
            @pl.when(not_edge)
            def _():
                in_copy(a).wait_recv()
                part[a] = (part[a].astype(f32) + inb[a].astype(f32)).astype(bf16)

            @pl.when(mid)
            def _():
                ex_copy(a).start()

            @pl.when(jnp.logical_and(not_mid, not_edge))
            def _():
                in_copy(a).start()

        b = j - 2 * lag

        @pl.when(jnp.logical_and(b >= 0, b < nch))
        def _():
            @pl.when(mid)
            def _():
                ex_copy(b).wait_recv()
                tot[b] = (part[b].astype(f32) + exb[b].astype(f32)).astype(bf16)

                @pl.when(not_edge)
                def _():
                    out_copy(b).start()

        e = j - 3 * lag

        @pl.when(e >= 0)
        def _():
            @pl.when(not_mid)
            def _():
                out_copy(e).wait_recv()

                @pl.when(not_edge)
                def _():
                    out_copy(e).start()

            pltpu.make_async_copy(tot.at[e], t_hbm.at[e], tsem.at[e]).start()
            pass_d(e)

        return carry

    lax.fori_loop(0, nch + 3 * lag, right_step, 0)

    def square(k, carry):
        t = tot[k].astype(f32)
        return carry + jnp.sum(t * t, axis=0, keepdims=True)

    norm_row = lax.fori_loop(0, nch, square, jnp.zeros((1, chunk), f32))
    s_ref[1:2, :] = total(1, jnp.sum(norm_row, axis=1, keepdims=True) / nr)

    lax.fori_loop(0, nch, drain_og, 0)
    for d in range(1, nc):
        act_copy(d).wait_send()
    for d in range(1, nx):
        remote(ld4.at[par, x], ld4.at[par, x], l3s.at[d - 1], l3r.at[d - 1], mate).wait_send()
    remote(ld4.at[par], ld4.at[par], l4.at[0], l4.at[1], mate).wait_send()
    for t in range(2):
        for d in range(1, nc):
            remote(sc.at[t, c], sc.at[t, c], cs.at[t, d - 1], cr.at[t, d - 1], mate).wait_send()
        for d in range(1, nr):
            remote(sr.at[t, r], sr.at[t, r], rs.at[t, d - 1], rr.at[t, d - 1], inn).wait_send()

    def drain_right(k, carry):
        pltpu.make_async_copy(tot.at[k], t_hbm.at[k], tsem.at[k]).wait()

        @pl.when(not_mid)
        def _():
            in_copy(k).wait_send()

        @pl.when(mid)
        def _():
            ex_copy(k).wait_send()

        @pl.when(not_edge)
        def _():
            out_copy(k).wait_send()
        return carry

    lax.fori_loop(0, nch, drain_right, 0)


def final_kernel(nch, chunk, s_ref, w_ref, l_ref, ldr_ref, ln_ref, r_ref, t_ref, o_ref):
    s1 = s_ref[0:1, 0:1]
    s2 = s_ref[1:2, 0:1]
    for k in range(nch):
        cols = slice(k * chunk, (k + 1) * chunk)
        rj = r_ref[cols, :]
        out = w_ref[:, cols].astype(f32) - mm_nt(l_ref[...], rj) - s1 * mm_nt(ldr_ref[...], rj)
        o_ref[:, cols] = (out - s2 * mm(ln_ref[...], t_ref[k])).astype(bf16)


def body(nr, nc, activations, out_grads, matrix, left, right):
    rows, cols = matrix.shape
    rank = left.shape[1]
    ctok = activations.shape[0]
    rtok = out_grads.shape[0]
    chunk = pick(cols, 512, 128)
    nch = cols // chunk
    tile = pick(rows, 256, 16)
    nx = nc // 2
    q = rows // nc
    dma = pltpu.SemaphoreType.DMA
    any_spec = pl.BlockSpec(memory_space=pl.ANY)
    vmem = pl.BlockSpec(memory_space=pltpu.VMEM)
    px = max(nx - 1, 1)
    pr = max(nr - 1, 1)
    pc = max(nc - 1, 1)
    left_new, left_round, right_t, steps = pl.pallas_call(
        functools.partial(main_kernel, nr, nc, nch, chunk, tile),
        out_shape=(
            jax.ShapeDtypeStruct((rows, rank), bf16),
            jax.ShapeDtypeStruct((rows, rank), bf16),
            jax.ShapeDtypeStruct((nch, rank, chunk), bf16),
            jax.ShapeDtypeStruct((2, 128), f32),
        ),
        in_specs=[any_spec, any_spec, any_spec, vmem, vmem],
        out_specs=(vmem, vmem, any_spec, vmem),
        scratch_shapes=[
            pltpu.VMEM((nch, rows, chunk), f32),
            pltpu.VMEM((2, rows, chunk), bf16),
            pltpu.VMEM((nch, nr, rtok, chunk), bf16),
            pltpu.VMEM((nc, ctok, rows), bf16),
            pltpu.VMEM((rows, nc * ctok), bf16),
            pltpu.VMEM((rows, rank), f32),
            pltpu.VMEM((2, nx, q, rank), bf16),
            pltpu.VMEM((nx, q, rank), bf16),
            pltpu.VMEM((px, q, rank), bf16),
            pltpu.VMEM((px, q, rank), bf16),
            pltpu.VMEM((2, nx, q, rank), bf16),
            pltpu.VMEM((rows // tile, rank, tile), bf16),
            pltpu.VMEM((nch, rank, chunk), bf16),
            pltpu.VMEM((nch, rank, chunk), bf16),
            pltpu.VMEM((nch, rank, chunk), bf16),
            pltpu.VMEM((nch, rank, chunk), bf16),
            pltpu.VMEM((rank, chunk), f32),
            pltpu.VMEM((8, chunk), f32),
            pltpu.VMEM((2, nc, 8, 128), f32),
            pltpu.VMEM((2, nr, 8, 128), f32),
            dma((2,)), dma((nch,)), dma, dma((pc,)), dma((pc,)),
            dma((nch, pr)), dma((nch, pr)), dma((nch, pr)), dma((nch, pr)),
            dma((2,)), dma((px,)), dma((px,)), dma((px,)), dma((px,)), dma((2,)),
            dma((2, pc)), dma((2, pc)), dma((2, pr)), dma((2, pr)),
            dma((nch,)), dma((nch,)), dma((nch,)), dma((nch,)), dma((nch,)), dma((nch,)), dma((nch,)),
        ],
        compiler_params=pltpu.CompilerParams(
            collective_id=0, has_side_effects=True, vmem_limit_bytes=66_500_000
        ),
        name="factor_steps",
    )(activations, out_grads, matrix, left, right)
    ft = pick(rows, 256, 16)
    block = lambda width: pl.BlockSpec((ft, width), lambda i: (i, 0))
    residual = pl.pallas_call(
        functools.partial(final_kernel, nch, chunk),
        grid=(rows // ft,),
        out_shape=jax.ShapeDtypeStruct((rows, cols), bf16),
        in_specs=[
            vmem, block(cols), block(rank), block(rank), block(rank), vmem, vmem,
        ],
        out_specs=block(cols),
        compiler_params=pltpu.CompilerParams(vmem_limit_bytes=50_000_000),
        name="residual",
    )(steps, matrix, left, left_round, left_new, right, right_t)
    descent = right_t.transpose(0, 2, 1).reshape(cols, rank).astype(f32)
    right_new = (right.astype(f32) + steps[1, 0] * descent).astype(bf16)
    return (left_new, right_new, residual)


def solution(mesh):
    placed = (
        P(("grp", "col"), "row"),
        P(("grp", "row"), "col"),
        P(("grp", "row"), "col"),
        P(("grp", "row"), None),
        P(("grp", "col"), None),
    )
    return jax.shard_map(
        functools.partial(body, mesh.shape["row"], mesh.shape["col"]),
        mesh=mesh,
        in_specs=placed,
        out_specs=(P(("grp", "row"), None), P(("grp", "col"), None), P(("grp", "row"), "col")),
        check_vma=False,
    )
```

```python
import functools

import jax
import jax.numpy as jnp
from jax import lax
from jax.experimental import pallas as pl
from jax.experimental.pallas import tpu as pltpu
from jax.sharding import PartitionSpec as P

epsilon = 1e-06
CHUNK = 256
TILE = 512
SPAN = 3
f32 = jnp.float32
bf16 = jnp.bfloat16
MESH = pl.DeviceIdType.MESH


def pick(extent, cap, unit):
    best = unit
    for size in range(unit, cap + 1, unit):
        if extent % size == 0:
            best = size
    return best


def mm(a, b):
    return jnp.dot(a, b, preferred_element_type=f32)


def main_kernel(
    nr, nc, nch, chunk, tile,
    act_hbm, og_hbm, w_hbm, l_ref, r_ref,
    ln_ref, ldr_ref, t_hbm, rt_hbm, s_ref,
    fisher, wbuf, ogb, actb, actt, rt, lpart, lsend, lr1, lh, lr2, ld4, lnt,
    part, inb, exb, tot, acc, sc, sr,
    wsem, ogsem, asem, act_s, act_r, up_s, up_r, dn_s, dn_r,
    l1, l2s, l2r, l3s, l3r, l4, cs, cr, rs, rr,
    in_s, in_r, ex_s, ex_r, out_s, out_r, tsem, rtsem,
):
    g = lax.axis_index("grp")
    r = lax.axis_index("row")
    c = lax.axis_index("col")
    nx = nc // 2
    rows = l_ref.shape[0]
    q = rows // nc
    nt = rows // tile
    lanes = pick(rows, 256, 128)

    def at(row, col):
        return (g, row, col)

    def remote(src, dst, ss, rs_, dev):
        return pltpu.make_async_remote_copy(
            src_ref=src, dst_ref=dst, send_sem=ss, recv_sem=rs_, device_id=dev, device_id_type=MESH
        )

    def w_copy(k, slot):
        cols = pl.ds(pl.multiple_of(k * chunk, 128), chunk)
        return pltpu.make_async_copy(w_hbm.at[:, cols], wbuf.at[slot], wsem.at[slot])

    def og_local(k):
        cols = pl.ds(pl.multiple_of(k * chunk, 128), chunk)
        return pltpu.make_async_copy(og_hbm.at[:, cols], ogb.at[k, r], ogsem.at[k])

    act_local = pltpu.make_async_copy(act_hbm, actb.at[c], asem)
    act_local.start()

    def start_og(k, carry):
        og_local(k).start()
        return carry

    lax.fori_loop(0, nch, start_og, 0)
    w_copy(0, 0).start()

    bar = pltpu.get_barrier_semaphore()
    for d in range(1, nr):
        pl.semaphore_signal(bar, inc=1, device_id=at(lax.rem(r + d, nr), c), device_id_type=MESH)
    for d in range(1, nc):
        pl.semaphore_signal(bar, inc=1, device_id=at(r, lax.rem(c + d, nc)), device_id_type=MESH)
    pl.semaphore_wait(bar, nr + nc - 2)

    act_local.wait()

    def act_copy(d):
        return remote(actb.at[c], actb.at[c], act_s.at[d - 1], act_r.at[d - 1], at(r, lax.rem(c + d, nc)))

    for d in range(1, nc):
        act_copy(d).start()

    def up_copy(k, s):
        blk = jnp.maximum(r - s, 0)
        return remote(ogb.at[k, blk], ogb.at[k, blk], up_s.at[k, s], up_r.at[k, s], at(jnp.minimum(r + 1, nr - 1), c))

    def dn_copy(k, s):
        blk = jnp.minimum(r + s, nr - 1)
        return remote(ogb.at[k, blk], ogb.at[k, blk], dn_s.at[k, s], dn_r.at[k, s], at(jnp.maximum(r - 1, 0), c))

    def up_sends(s):
        return jnp.logical_and(r - s >= 0, r + 1 < nr)

    def dn_sends(s):
        return jnp.logical_and(r + s < nr, r >= 1)

    def up_wait(k, s):
        blk = jnp.maximum(r - 1 - s, 0)
        remote(ogb.at[k, blk], ogb.at[k, blk], up_s.at[k, s], up_r.at[k, s], at(jnp.minimum(r + 1, nr - 1), c)).wait_recv()

    def dn_wait(k, s):
        blk = jnp.minimum(r + 1 + s, nr - 1)
        remote(ogb.at[k, blk], ogb.at[k, blk], dn_s.at[k, s], dn_r.at[k, s], at(jnp.maximum(r - 1, 0), c)).wait_recv()

    lpart[...] = jnp.zeros_like(lpart)
    acc[...] = jnp.zeros_like(acc)

    def rows_at(i):
        return pl.ds(i * tile, tile)

    def cols_at(k):
        return pl.ds(pl.multiple_of(k * chunk, chunk), chunk)

    def pass_a(k):
        slot = lax.rem(k, 2)
        w_copy(lax.rem(k + 1, nch), lax.rem(k + 1, 2)).start()
        w_copy(k, slot).wait()

        og = ogb[k].reshape(-1, chunk)
        rj = r_ref[cols_at(k), :]
        for i in range(nt):
            rw = rows_at(i)
            grad = mm(actt[rw, :], og)
            w = wbuf[slot, rw, :].astype(f32)
            wg = w * grad
            fish = 1.0 + wg * wg
            fisher[k, rw, :] = fish
            early = w - mm(l_ref[rw, :], rt[k])
            lpart[rw, :] += mm((fish * early).astype(bf16), rj)

    def turn_right(k, carry):
        rt[k] = r_ref[cols_at(k), :].astype(f32).T.astype(bf16)
        pltpu.make_async_copy(rt.at[k], rt_hbm.at[k], rtsem.at[k]).start()
        return carry

    def gather_step(j, carry):
        @pl.when(j < nch)
        def _():
            og_local(j).wait()

            @pl.when(up_sends(0))
            def _():
                up_copy(j, 0).start()

            @pl.when(dn_sends(0))
            def _():
                dn_copy(j, 0).start()

        for s in range(1, nr):
            k = j - s

            @pl.when(jnp.logical_and(k >= 0, k < nch))
            def _():
                @pl.when(r - s >= 0)
                def _():
                    up_wait(k, s - 1)

                @pl.when(up_sends(s))
                def _():
                    up_copy(k, s).start()

                @pl.when(r + s < nr)
                def _():
                    dn_wait(k, s - 1)

                @pl.when(dn_sends(s))
                def _():
                    dn_copy(k, s).start()

        @pl.when(j == nr - 1)
        def _():
            for d in range(1, nc):
                src = lax.rem(c + nc - d, nc)
                remote(actb.at[src], actb.at[src], act_s.at[d - 1], act_r.at[d - 1], at(r, src)).wait_recv()

            def turn(i, carry):
                rw = pl.ds(pl.multiple_of(i * lanes, lanes), lanes)
                block = actb[:, :, rw].reshape(-1, lanes)
                actt[rw, :] = block.astype(f32).T.astype(bf16)
                return carry

            lax.fori_loop(0, rows // lanes, turn, 0)
            lax.fori_loop(0, nch, turn_right, 0)

        @pl.when(j >= nr - 1)
        def _():
            pass_a(j - (nr - 1))

        return carry

    lax.fori_loop(0, nch + nr - 1, gather_step, 0)

    def drain_og(k, carry):
        for s in range(nr - 1):
            @pl.when(up_sends(s))
            def _():
                up_copy(k, s).wait_send()

            @pl.when(dn_sends(s))
            def _():
                dn_copy(k, s).wait_send()
        return carry

    par = lax.rem(c, 2)
    x = c // 2
    mate = at(r, c + 1 - 2 * par)
    for k in range(nc):
        lsend[k % 2, k // 2] = lpart[k * q:(k + 1) * q, :].astype(bf16)
    one = remote(lsend.at[1 - par], lr1, l1.at[0], l1.at[1], mate)
    one.start()
    one.wait()

    def own_rows(xx):
        return lpart[pl.ds(pl.multiple_of((2 * xx + par) * q, 8), q), :] + lr1[xx].astype(f32)

    for d in range(1, nx):
        xx = lax.rem(x + d, nx)
        lh[d - 1] = own_rows(xx).astype(bf16)
        remote(lh.at[d - 1], lr2.at[d - 1], l2s.at[d - 1], l2r.at[d - 1], at(r, 2 * xx + par)).start()
    desc = own_rows(x)
    for d in range(1, nx):
        xx = lax.rem(x + d, nx)
        remote(lh.at[d - 1], lr2.at[d - 1], l2s.at[d - 1], l2r.at[d - 1], at(r, 2 * xx + par)).wait()
        desc = desc + lr2[d - 1].astype(f32)
    norm = jnp.sum(jnp.sum(desc * desc, axis=0, keepdims=True), axis=1, keepdims=True)
    ld4[par, x] = desc.astype(bf16)
    for d in range(1, nx):
        xx = lax.rem(x + d, nx)
        remote(ld4.at[par, x], ld4.at[par, x], l3s.at[d - 1], l3r.at[d - 1], at(r, 2 * xx + par)).start()
    for d in range(1, nx):
        xx = lax.rem(x + nx - d, nx)
        got = remote(ld4.at[par, xx], ld4.at[par, xx], l3s.at[d - 1], l3r.at[d - 1], at(r, 2 * xx + par))
        got.wait_recv()
    remote(ld4.at[par], ld4.at[par], l4.at[0], l4.at[1], mate).start()
    remote(ld4.at[1 - par], ld4.at[1 - par], l4.at[0], l4.at[1], mate).wait_recv()
    for k in range(nc):
        lpart[k * q:(k + 1) * q, :] = ld4[k % 2, k // 2].astype(f32)

    for i in range(nt):
        ldr_ref[rows_at(i), :] = lpart[rows_at(i), :].astype(bf16)

    def curve(k, lhs_ref, rhs):
        found = acc[...]
        for i in range(nt):
            rw = rows_at(i)
            image = mm(lhs_ref[rw, :], rhs)
            weighted = fisher[k, rw, :] * image * image
            found = found + jnp.sum(weighted.reshape(tile // 8, 8, chunk), axis=0)
        acc[...] = found

    def pass_b(k, carry):
        curve(k, ldr_ref, rt[k])
        return carry

    lax.fori_loop(0, nch, pass_b, 0)

    def total(t, norm_part):
        bend = jnp.sum(jnp.sum(acc[...], axis=0, keepdims=True), axis=1, keepdims=True)
        top = lax.broadcasted_iota(jnp.int32, (8, 128), 0) == 0
        sc[t, c] = jnp.where(top, jnp.broadcast_to(bend, (8, 128)), jnp.broadcast_to(norm_part, (8, 128)))
        for d in range(1, nc):
            remote(sc.at[t, c], sc.at[t, c], cs.at[t, d - 1], cr.at[t, d - 1], at(r, lax.rem(c + d, nc))).start()
        for d in range(1, nc):
            src = lax.rem(c + nc - d, nc)
            remote(sc.at[t, src], sc.at[t, src], cs.at[t, d - 1], cr.at[t, d - 1], at(r, src)).wait_recv()
        sr[t, r] = jnp.sum(sc[t], axis=0)
        for d in range(1, nr):
            remote(sr.at[t, r], sr.at[t, r], rs.at[t, d - 1], rr.at[t, d - 1], at(lax.rem(r + d, nr), c)).start()
        for d in range(1, nr):
            src = lax.rem(r + nr - d, nr)
            remote(sr.at[t, src], sr.at[t, src], rs.at[t, d - 1], rr.at[t, d - 1], at(src, c)).wait_recv()
        both = jnp.sum(sr[t], axis=0)
        return both[1:2, :] / (both[0:1, :] + epsilon)

    s_ref[0:1, :] = total(0, norm)

    for i in range(nt):
        rw = rows_at(i)
        new = (l_ref[rw, :].astype(f32) + s_ref[0:1, 0:1] * lpart[rw, :]).astype(bf16)
        ln_ref[rw, :] = new
        lnt[i] = new.astype(f32).T.astype(bf16)
    acc[...] = jnp.zeros_like(acc)

    half = nr // 2
    lower = r < half
    inn = at(jnp.where(lower, r + 1, r - 1), c)
    outn = at(jnp.where(lower, jnp.maximum(r - 1, 0), jnp.minimum(r + 1, nr - 1)), c)
    mid = jnp.logical_or(r == half - 1, r == half)
    edge = jnp.logical_or(r == 0, r == nr - 1)
    not_mid = jnp.logical_not(mid)
    not_edge = jnp.logical_not(edge)

    def in_copy(k):
        return remote(part.at[k], inb.at[k], in_s.at[k], in_r.at[k], inn)

    def ex_copy(k):
        return remote(part.at[k], exb.at[k], ex_s.at[k], ex_r.at[k], inn)

    def out_copy(k):
        return remote(tot.at[k], tot.at[k], out_s.at[k], out_r.at[k], outn)

    def pass_c(k):
        slot = lax.rem(k + nch, 2)

        @pl.when(k + 1 < nch)
        def _():
            w_copy(k + 1, lax.rem(k + 1 + nch, 2)).start()

        w_copy(k, slot).wait()
        moved = jnp.zeros((l_ref.shape[1], chunk), f32)
        for i in range(nt):
            rw = rows_at(i)
            later = wbuf[slot, rw, :].astype(f32) - mm(l_ref[rw, :], rt[k])
            later = later - s_ref[0:1, 0:1] * mm(ldr_ref[rw, :], rt[k])
            moved = moved + mm(lnt[i], (fisher[k, rw, :] * later).astype(bf16))
        part[k] = moved.astype(bf16)

    def pass_d(k):
        curve(k, ln_ref, tot[k])

    lag = 2

    def right_step(j, carry):
        @pl.when(j < nch)
        def _():
            pass_c(j)

            @pl.when(jnp.logical_and(edge, not_mid))
            def _():
                in_copy(j).start()

        a = j - lag

        @pl.when(jnp.logical_and(a >= 0, a < nch))
        def _():
            @pl.when(not_edge)
            def _():
                in_copy(a).wait_recv()
                part[a] = (part[a].astype(f32) + inb[a].astype(f32)).astype(bf16)

            @pl.when(mid)
            def _():
                ex_copy(a).start()

            @pl.when(jnp.logical_and(not_mid, not_edge))
            def _():
                in_copy(a).start()

        b = j - 2 * lag

        @pl.when(jnp.logical_and(b >= 0, b < nch))
        def _():
            @pl.when(mid)
            def _():
                ex_copy(b).wait_recv()
                tot[b] = (part[b].astype(f32) + exb[b].astype(f32)).astype(bf16)

                @pl.when(not_edge)
                def _():
                    out_copy(b).start()

        e = j - 3 * lag

        @pl.when(e >= 0)
        def _():
            @pl.when(not_mid)
            def _():
                out_copy(e).wait_recv()

                @pl.when(not_edge)
                def _():
                    out_copy(e).start()

            pltpu.make_async_copy(tot.at[e], t_hbm.at[e], tsem.at[e]).start()
            pass_d(e)

        return carry

    lax.fori_loop(0, nch + 3 * lag, right_step, 0)

    def square(k, carry):
        t = tot[k].astype(f32)
        return carry + jnp.sum(t * t, axis=0, keepdims=True)

    norm_row = lax.fori_loop(0, nch, square, jnp.zeros((1, chunk), f32))
    s_ref[1:2, :] = total(1, jnp.sum(norm_row, axis=1, keepdims=True) / nr)

    lax.fori_loop(0, nch, drain_og, 0)
    for d in range(1, nc):
        act_copy(d).wait_send()
    for d in range(1, nx):
        remote(ld4.at[par, x], ld4.at[par, x], l3s.at[d - 1], l3r.at[d - 1], mate).wait_send()
    remote(ld4.at[par], ld4.at[par], l4.at[0], l4.at[1], mate).wait_send()
    for t in range(2):
        for d in range(1, nc):
            remote(sc.at[t, c], sc.at[t, c], cs.at[t, d - 1], cr.at[t, d - 1], mate).wait_send()
        for d in range(1, nr):
            remote(sr.at[t, r], sr.at[t, r], rs.at[t, d - 1], rr.at[t, d - 1], inn).wait_send()

    def drain_right(k, carry):
        pltpu.make_async_copy(tot.at[k], t_hbm.at[k], tsem.at[k]).wait()
        pltpu.make_async_copy(rt.at[k], rt_hbm.at[k], rtsem.at[k]).wait()

        @pl.when(not_mid)
        def _():
            in_copy(k).wait_send()

        @pl.when(mid)
        def _():
            ex_copy(k).wait_send()

        @pl.when(not_edge)
        def _():
            out_copy(k).wait_send()
        return carry

    lax.fori_loop(0, nch, drain_right, 0)


def final_kernel(span, chunk, tile, s_ref, w_ref, l_ref, ldr_ref, ln_ref, r_ref, rt_ref, t_ref, o_ref, rn_ref):
    s1 = s_ref[0:1, 0:1]
    s2 = s_ref[1:2, 0:1]
    for k in range(span):
        cols = slice(k * chunk, (k + 1) * chunk)
        rn_ref[cols, :] = (r_ref[cols, :].astype(f32) + s2 * t_ref[k].astype(f32).T).astype(bf16)

        for i in range(l_ref.shape[0] // tile):
            rw = slice(i * tile, (i + 1) * tile)
            out = w_ref[rw, cols].astype(f32) - mm(l_ref[rw, :], rt_ref[k]) - s1 * mm(ldr_ref[rw, :], rt_ref[k])
            o_ref[rw, cols] = (out - s2 * mm(ln_ref[rw, :], t_ref[k])).astype(bf16)


def body(nr, nc, activations, out_grads, matrix, left, right):
    rows, cols = matrix.shape
    rank = left.shape[1]
    ctok = activations.shape[0]
    rtok = out_grads.shape[0]
    chunk = pick(cols, CHUNK, 128)
    nch = cols // chunk
    tile = pick(rows, TILE, 16)
    nx = nc // 2
    q = rows // nc
    dma = pltpu.SemaphoreType.DMA
    any_spec = pl.BlockSpec(memory_space=pl.ANY)
    vmem = pl.BlockSpec(memory_space=pltpu.VMEM)
    px = max(nx - 1, 1)
    pr = max(nr - 1, 1)
    pc = max(nc - 1, 1)
    left_new, left_round, descent_t, right_t, steps = pl.pallas_call(
        functools.partial(main_kernel, nr, nc, nch, chunk, tile),
        out_shape=(
            jax.ShapeDtypeStruct((rows, rank), bf16),
            jax.ShapeDtypeStruct((rows, rank), bf16),
            jax.ShapeDtypeStruct((nch, rank, chunk), bf16),
            jax.ShapeDtypeStruct((nch, rank, chunk), bf16),
            jax.ShapeDtypeStruct((2, 128), f32),
        ),
        in_specs=[any_spec, any_spec, any_spec, vmem, vmem],
        out_specs=(vmem, vmem, any_spec, any_spec, vmem),
        scratch_shapes=[
            pltpu.VMEM((nch, rows, chunk), f32),
            pltpu.VMEM((2, rows, chunk), bf16),
            pltpu.VMEM((nch, nr, rtok, chunk), bf16),
            pltpu.VMEM((nc, ctok, rows), bf16),
            pltpu.VMEM((rows, nc * ctok), bf16),
            pltpu.VMEM((nch, rank, chunk), bf16),
            pltpu.VMEM((rows, rank), f32),
            pltpu.VMEM((2, nx, q, rank), bf16),
            pltpu.VMEM((nx, q, rank), bf16),
            pltpu.VMEM((px, q, rank), bf16),
            pltpu.VMEM((px, q, rank), bf16),
            pltpu.VMEM((2, nx, q, rank), bf16),
            pltpu.VMEM((rows // tile, rank, tile), bf16),
            pltpu.VMEM((nch, rank, chunk), bf16),
            pltpu.VMEM((nch, rank, chunk), bf16),
            pltpu.VMEM((nch, rank, chunk), bf16),
            pltpu.VMEM((nch, rank, chunk), bf16),
            pltpu.VMEM((8, chunk), f32),
            pltpu.VMEM((2, nc, 8, 128), f32),
            pltpu.VMEM((2, nr, 8, 128), f32),
            dma((2,)), dma((nch,)), dma, dma((pc,)), dma((pc,)),
            dma((nch, pr)), dma((nch, pr)), dma((nch, pr)), dma((nch, pr)),
            dma((2,)), dma((px,)), dma((px,)), dma((px,)), dma((px,)), dma((2,)),
            dma((2, pc)), dma((2, pc)), dma((2, pr)), dma((2, pr)),
            dma((nch,)), dma((nch,)), dma((nch,)), dma((nch,)), dma((nch,)), dma((nch,)), dma((nch,)), dma((nch,)),
        ],
        compiler_params=pltpu.CompilerParams(
            collective_id=0, has_side_effects=True, vmem_limit_bytes=66_500_000
        ),
        name="factor_steps",
    )(activations, out_grads, matrix, left, right)
    span = pick(nch, SPAN, 1)
    wide = pl.BlockSpec((rows, span * chunk), lambda i: (0, i))
    tall = pl.BlockSpec((span * chunk, rank), lambda i: (i, 0))
    turned = pl.BlockSpec((span, rank, chunk), lambda i: (i, 0, 0))
    residual, right_new = pl.pallas_call(
        functools.partial(final_kernel, span, chunk, tile),
        grid=(nch // span,),
        out_shape=(
            jax.ShapeDtypeStruct((rows, cols), bf16),
            jax.ShapeDtypeStruct((cols, rank), bf16),
        ),
        in_specs=[vmem, wide, vmem, vmem, vmem, tall, turned, turned],
        out_specs=(wide, tall),
        compiler_params=pltpu.CompilerParams(vmem_limit_bytes=50_000_000),
        name="residual",
    )(steps, matrix, left, left_round, left_new, right, right_t, descent_t)
    return (left_new, right_new, residual)


def solution(mesh):
    placed = (
        P(("grp", "col"), "row"),
        P(("grp", "row"), "col"),
        P(("grp", "row"), "col"),
        P(("grp", "row"), None),
        P(("grp", "col"), None),
    )
    return jax.shard_map(
        functools.partial(body, mesh.shape["row"], mesh.shape["col"]),
        mesh=mesh,
        in_specs=placed,
        out_specs=(P(("grp", "row"), None), P(("grp", "col"), None), P(("grp", "row"), "col")),
        check_vma=False,
    )
```

```python
import functools

import jax
import jax.numpy as jnp
from jax import lax
from jax.experimental import pallas as pl
from jax.experimental.pallas import tpu as pltpu
from jax.sharding import PartitionSpec as P

epsilon = 1e-06
CHUNK = 256
TILE = 512
SPAN = 3
f32 = jnp.float32
bf16 = jnp.bfloat16
MESH = pl.DeviceIdType.MESH


def pick(extent, cap, unit):
    best = unit
    for size in range(unit, cap + 1, unit):
        if extent % size == 0:
            best = size
    return best


def mm(a, b):
    return jnp.dot(a, b, preferred_element_type=f32)


def main_kernel(
    nr, nc, nch, chunk, tile,
    act_hbm, og_hbm, w_hbm, l_hbm, r_hbm,
    ln_hbm, ldr_hbm, t_hbm, rt_hbm, s_ref,
    l_ref, r_ref, ln_ref, ldr_ref,
    fisher, wbuf, ogb, actb, actt, rt, lpart, lsend, lr1, lh, lr2, ld4, lnt,
    part, inb, exb, tot, acc, sc, sr,
    wsem, ogsem, asem, act_s, act_r, up_s, up_r, dn_s, dn_r,
    l1, l2s, l2r, l3s, l3r, l4, cs, cr, rs, rr,
    in_s, in_r, ex_s, ex_r, out_s, out_r, tsem, rtsem, iosem,
):
    g = lax.axis_index("grp")
    r = lax.axis_index("row")
    c = lax.axis_index("col")
    nx = nc // 2
    rows = l_ref.shape[0]
    q = rows // nc
    nt = rows // tile
    lanes = pick(rows, 256, 128)

    def at(row, col):
        return (g, row, col)

    def remote(src, dst, ss, rs_, dev):
        return pltpu.make_async_remote_copy(
            src_ref=src, dst_ref=dst, send_sem=ss, recv_sem=rs_, device_id=dev, device_id_type=MESH
        )

    def w_copy(k, slot):
        cols = pl.ds(pl.multiple_of(k * chunk, 128), chunk)
        return pltpu.make_async_copy(w_hbm.at[:, cols], wbuf.at[slot], wsem.at[slot])

    def og_local(k):
        cols = pl.ds(pl.multiple_of(k * chunk, 128), chunk)
        return pltpu.make_async_copy(og_hbm.at[:, cols], ogb.at[k, r], ogsem.at[k])

    act_local = pltpu.make_async_copy(act_hbm, actb.at[c], asem)
    act_local.start()

    def start_og(k, carry):
        og_local(k).start()
        return carry

    lax.fori_loop(0, nch, start_og, 0)
    w_copy(0, 0).start()
    l_in = pltpu.make_async_copy(l_hbm, l_ref, iosem.at[0])
    r_in = pltpu.make_async_copy(r_hbm, r_ref, iosem.at[1])
    ldr_out = pltpu.make_async_copy(ldr_ref, ldr_hbm, iosem.at[2])
    ln_out = pltpu.make_async_copy(ln_ref, ln_hbm, iosem.at[3])
    l_in.start()
    r_in.start()

    bar = pltpu.get_barrier_semaphore()
    for d in range(1, nr):
        pl.semaphore_signal(bar, inc=1, device_id=at(lax.rem(r + d, nr), c), device_id_type=MESH)
    for d in range(1, nc):
        pl.semaphore_signal(bar, inc=1, device_id=at(r, lax.rem(c + d, nc)), device_id_type=MESH)
    pl.semaphore_wait(bar, nr + nc - 2)

    act_local.wait()

    def act_copy(d):
        return remote(actb.at[c], actb.at[c], act_s.at[d - 1], act_r.at[d - 1], at(r, lax.rem(c + d, nc)))

    for d in range(1, nc):
        act_copy(d).start()

    def up_copy(k, s):
        blk = jnp.maximum(r - s, 0)
        return remote(ogb.at[k, blk], ogb.at[k, blk], up_s.at[k, s], up_r.at[k, s], at(jnp.minimum(r + 1, nr - 1), c))

    def dn_copy(k, s):
        blk = jnp.minimum(r + s, nr - 1)
        return remote(ogb.at[k, blk], ogb.at[k, blk], dn_s.at[k, s], dn_r.at[k, s], at(jnp.maximum(r - 1, 0), c))

    def up_sends(s):
        return jnp.logical_and(r - s >= 0, r + 1 < nr)

    def dn_sends(s):
        return jnp.logical_and(r + s < nr, r >= 1)

    def up_wait(k, s):
        blk = jnp.maximum(r - 1 - s, 0)
        remote(ogb.at[k, blk], ogb.at[k, blk], up_s.at[k, s], up_r.at[k, s], at(jnp.minimum(r + 1, nr - 1), c)).wait_recv()

    def dn_wait(k, s):
        blk = jnp.minimum(r + 1 + s, nr - 1)
        remote(ogb.at[k, blk], ogb.at[k, blk], dn_s.at[k, s], dn_r.at[k, s], at(jnp.maximum(r - 1, 0), c)).wait_recv()

    lpart[...] = jnp.zeros_like(lpart)
    l_in.wait()
    r_in.wait()
    acc[...] = jnp.zeros_like(acc)

    def rows_at(i):
        return pl.ds(i * tile, tile)

    def cols_at(k):
        return pl.ds(pl.multiple_of(k * chunk, chunk), chunk)

    def pass_a(k):
        slot = lax.rem(k, 2)
        w_copy(lax.rem(k + 1, nch), lax.rem(k + 1, 2)).start()
        w_copy(k, slot).wait()

        og = ogb[k].reshape(-1, chunk)
        rj = r_ref[cols_at(k), :]
        for i in range(nt):
            rw = rows_at(i)
            grad = mm(actt[rw, :], og)
            w = wbuf[slot, rw, :].astype(f32)
            wg = w * grad
            fish = 1.0 + wg * wg
            fisher[k, rw, :] = fish
            early = w - mm(l_ref[rw, :], rt[k])
            lpart[rw, :] += mm((fish * early).astype(bf16), rj)

    def turn_right(k, carry):
        rt[k] = r_ref[cols_at(k), :].astype(f32).T.astype(bf16)
        pltpu.make_async_copy(rt.at[k], rt_hbm.at[k], rtsem.at[k]).start()
        return carry

    def gather_step(j, carry):
        @pl.when(j < nch)
        def _():
            og_local(j).wait()

            @pl.when(up_sends(0))
            def _():
                up_copy(j, 0).start()

            @pl.when(dn_sends(0))
            def _():
                dn_copy(j, 0).start()

        for s in range(1, nr):
            k = j - s

            @pl.when(jnp.logical_and(k >= 0, k < nch))
            def _():
                @pl.when(r - s >= 0)
                def _():
                    up_wait(k, s - 1)

                @pl.when(up_sends(s))
                def _():
                    up_copy(k, s).start()

                @pl.when(r + s < nr)
                def _():
                    dn_wait(k, s - 1)

                @pl.when(dn_sends(s))
                def _():
                    dn_copy(k, s).start()

        @pl.when(j == nr - 1)
        def _():
            for d in range(1, nc):
                src = lax.rem(c + nc - d, nc)
                remote(actb.at[src], actb.at[src], act_s.at[d - 1], act_r.at[d - 1], at(r, src)).wait_recv()

            def turn(i, carry):
                rw = pl.ds(pl.multiple_of(i * lanes, lanes), lanes)
                block = actb[:, :, rw].reshape(-1, lanes)
                actt[rw, :] = block.astype(f32).T.astype(bf16)
                return carry

            lax.fori_loop(0, rows // lanes, turn, 0)
            lax.fori_loop(0, nch, turn_right, 0)

        @pl.when(j >= nr - 1)
        def _():
            pass_a(j - (nr - 1))

        return carry

    lax.fori_loop(0, nch + nr - 1, gather_step, 0)

    def drain_og(k, carry):
        for s in range(nr - 1):
            @pl.when(up_sends(s))
            def _():
                up_copy(k, s).wait_send()

            @pl.when(dn_sends(s))
            def _():
                dn_copy(k, s).wait_send()
        return carry

    par = lax.rem(c, 2)
    x = c // 2
    mate = at(r, c + 1 - 2 * par)
    for k in range(nc):
        lsend[k % 2, k // 2] = lpart[k * q:(k + 1) * q, :].astype(bf16)
    one = remote(lsend.at[1 - par], lr1, l1.at[0], l1.at[1], mate)
    one.start()
    one.wait()

    def own_rows(xx):
        return lpart[pl.ds(pl.multiple_of((2 * xx + par) * q, 8), q), :] + lr1[xx].astype(f32)

    for d in range(1, nx):
        xx = lax.rem(x + d, nx)
        lh[d - 1] = own_rows(xx).astype(bf16)
        remote(lh.at[d - 1], lr2.at[d - 1], l2s.at[d - 1], l2r.at[d - 1], at(r, 2 * xx + par)).start()
    desc = own_rows(x)
    for d in range(1, nx):
        xx = lax.rem(x + d, nx)
        remote(lh.at[d - 1], lr2.at[d - 1], l2s.at[d - 1], l2r.at[d - 1], at(r, 2 * xx + par)).wait()
        desc = desc + lr2[d - 1].astype(f32)
    norm = jnp.sum(jnp.sum(desc * desc, axis=0, keepdims=True), axis=1, keepdims=True)
    ld4[par, x] = desc.astype(bf16)
    for d in range(1, nx):
        xx = lax.rem(x + d, nx)
        remote(ld4.at[par, x], ld4.at[par, x], l3s.at[d - 1], l3r.at[d - 1], at(r, 2 * xx + par)).start()
    for d in range(1, nx):
        xx = lax.rem(x + nx - d, nx)
        got = remote(ld4.at[par, xx], ld4.at[par, xx], l3s.at[d - 1], l3r.at[d - 1], at(r, 2 * xx + par))
        got.wait_recv()
    remote(ld4.at[par], ld4.at[par], l4.at[0], l4.at[1], mate).start()
    remote(ld4.at[1 - par], ld4.at[1 - par], l4.at[0], l4.at[1], mate).wait_recv()
    for k in range(nc):
        lpart[k * q:(k + 1) * q, :] = ld4[k % 2, k // 2].astype(f32)

    for i in range(nt):
        ldr_ref[rows_at(i), :] = lpart[rows_at(i), :].astype(bf16)
    ldr_out.start()

    def curve(k, lhs_ref, rhs):
        found = acc[...]
        for i in range(nt):
            rw = rows_at(i)
            image = mm(lhs_ref[rw, :], rhs)
            weighted = fisher[k, rw, :] * image * image
            found = found + jnp.sum(weighted.reshape(tile // 8, 8, chunk), axis=0)
        acc[...] = found

    def pass_b(k, carry):
        curve(k, ldr_ref, rt[k])
        return carry

    lax.fori_loop(0, nch, pass_b, 0)

    def total(t, norm_part):
        bend = jnp.sum(jnp.sum(acc[...], axis=0, keepdims=True), axis=1, keepdims=True)
        top = lax.broadcasted_iota(jnp.int32, (8, 128), 0) == 0
        sc[t, c] = jnp.where(top, jnp.broadcast_to(bend, (8, 128)), jnp.broadcast_to(norm_part, (8, 128)))
        for d in range(1, nc):
            remote(sc.at[t, c], sc.at[t, c], cs.at[t, d - 1], cr.at[t, d - 1], at(r, lax.rem(c + d, nc))).start()
        for d in range(1, nc):
            src = lax.rem(c + nc - d, nc)
            remote(sc.at[t, src], sc.at[t, src], cs.at[t, d - 1], cr.at[t, d - 1], at(r, src)).wait_recv()
        sr[t, r] = jnp.sum(sc[t], axis=0)
        for d in range(1, nr):
            remote(sr.at[t, r], sr.at[t, r], rs.at[t, d - 1], rr.at[t, d - 1], at(lax.rem(r + d, nr), c)).start()
        for d in range(1, nr):
            src = lax.rem(r + nr - d, nr)
            remote(sr.at[t, src], sr.at[t, src], rs.at[t, d - 1], rr.at[t, d - 1], at(src, c)).wait_recv()
        both = jnp.sum(sr[t], axis=0)
        return both[1:2, :] / (both[0:1, :] + epsilon)

    s_ref[0:1, :] = total(0, norm)

    for i in range(nt):
        rw = rows_at(i)
        new = (l_ref[rw, :].astype(f32) + s_ref[0:1, 0:1] * lpart[rw, :]).astype(bf16)
        ln_ref[rw, :] = new
        lnt[i] = new.astype(f32).T.astype(bf16)
    ln_out.start()
    acc[...] = jnp.zeros_like(acc)

    half = nr // 2
    lower = r < half
    inn = at(jnp.where(lower, r + 1, r - 1), c)
    outn = at(jnp.where(lower, jnp.maximum(r - 1, 0), jnp.minimum(r + 1, nr - 1)), c)
    mid = jnp.logical_or(r == half - 1, r == half)
    edge = jnp.logical_or(r == 0, r == nr - 1)
    not_mid = jnp.logical_not(mid)
    not_edge = jnp.logical_not(edge)

    def in_copy(k):
        return remote(part.at[k], inb.at[k], in_s.at[k], in_r.at[k], inn)

    def ex_copy(k):
        return remote(part.at[k], exb.at[k], ex_s.at[k], ex_r.at[k], inn)

    def out_copy(k):
        return remote(tot.at[k], tot.at[k], out_s.at[k], out_r.at[k], outn)

    def pass_c(k):
        slot = lax.rem(k + nch, 2)

        @pl.when(k + 1 < nch)
        def _():
            w_copy(k + 1, lax.rem(k + 1 + nch, 2)).start()

        w_copy(k, slot).wait()
        moved = jnp.zeros((l_ref.shape[1], chunk), f32)
        for i in range(nt):
            rw = rows_at(i)
            later = wbuf[slot, rw, :].astype(f32) - mm(l_ref[rw, :], rt[k])
            later = later - s_ref[0:1, 0:1] * mm(ldr_ref[rw, :], rt[k])
            moved = moved + mm(lnt[i], (fisher[k, rw, :] * later).astype(bf16))
        part[k] = moved.astype(bf16)

    def pass_d(k):
        curve(k, ln_ref, tot[k])

    lag = 2

    def right_step(j, carry):
        @pl.when(j < nch)
        def _():
            pass_c(j)

            @pl.when(jnp.logical_and(edge, not_mid))
            def _():
                in_copy(j).start()

        a = j - lag

        @pl.when(jnp.logical_and(a >= 0, a < nch))
        def _():
            @pl.when(not_edge)
            def _():
                in_copy(a).wait_recv()
                part[a] = (part[a].astype(f32) + inb[a].astype(f32)).astype(bf16)

            @pl.when(mid)
            def _():
                ex_copy(a).start()

            @pl.when(jnp.logical_and(not_mid, not_edge))
            def _():
                in_copy(a).start()

        b = j - 2 * lag

        @pl.when(jnp.logical_and(b >= 0, b < nch))
        def _():
            @pl.when(mid)
            def _():
                ex_copy(b).wait_recv()
                tot[b] = (part[b].astype(f32) + exb[b].astype(f32)).astype(bf16)

                @pl.when(not_edge)
                def _():
                    out_copy(b).start()

        e = j - 3 * lag

        @pl.when(e >= 0)
        def _():
            @pl.when(not_mid)
            def _():
                out_copy(e).wait_recv()

                @pl.when(not_edge)
                def _():
                    out_copy(e).start()

            pltpu.make_async_copy(tot.at[e], t_hbm.at[e], tsem.at[e]).start()
            pass_d(e)

        return carry

    lax.fori_loop(0, nch + 3 * lag, right_step, 0)

    def square(k, carry):
        t = tot[k].astype(f32)
        return carry + jnp.sum(t * t, axis=0, keepdims=True)

    norm_row = lax.fori_loop(0, nch, square, jnp.zeros((1, chunk), f32))
    s_ref[1:2, :] = total(1, jnp.sum(norm_row, axis=1, keepdims=True) / nr)

    lax.fori_loop(0, nch, drain_og, 0)
    for d in range(1, nc):
        act_copy(d).wait_send()
    for d in range(1, nx):
        remote(ld4.at[par, x], ld4.at[par, x], l3s.at[d - 1], l3r.at[d - 1], mate).wait_send()
    remote(ld4.at[par], ld4.at[par], l4.at[0], l4.at[1], mate).wait_send()
    for t in range(2):
        for d in range(1, nc):
            remote(sc.at[t, c], sc.at[t, c], cs.at[t, d - 1], cr.at[t, d - 1], mate).wait_send()
        for d in range(1, nr):
            remote(sr.at[t, r], sr.at[t, r], rs.at[t, d - 1], rr.at[t, d - 1], inn).wait_send()

    def drain_right(k, carry):
        pltpu.make_async_copy(tot.at[k], t_hbm.at[k], tsem.at[k]).wait()
        pltpu.make_async_copy(rt.at[k], rt_hbm.at[k], rtsem.at[k]).wait()

        @pl.when(not_mid)
        def _():
            in_copy(k).wait_send()

        @pl.when(mid)
        def _():
            ex_copy(k).wait_send()

        @pl.when(not_edge)
        def _():
            out_copy(k).wait_send()
        return carry

    lax.fori_loop(0, nch, drain_right, 0)
    ldr_out.wait()
    ln_out.wait()


def final_kernel(span, chunk, tile, s_ref, w_ref, l_ref, ldr_ref, ln_ref, r_ref, rt_ref, t_ref, o_ref, rn_ref):
    s1 = s_ref[0:1, 0:1]
    s2 = s_ref[1:2, 0:1]
    for k in range(span):
        cols = slice(k * chunk, (k + 1) * chunk)
        rn_ref[cols, :] = (r_ref[cols, :].astype(f32) + s2 * t_ref[k].astype(f32).T).astype(bf16)

        for i in range(l_ref.shape[0] // tile):
            rw = slice(i * tile, (i + 1) * tile)
            out = w_ref[rw, cols].astype(f32) - mm(l_ref[rw, :], rt_ref[k]) - s1 * mm(ldr_ref[rw, :], rt_ref[k])
            o_ref[rw, cols] = (out - s2 * mm(ln_ref[rw, :], t_ref[k])).astype(bf16)


def body(nr, nc, activations, out_grads, matrix, left, right):
    rows, cols = matrix.shape
    rank = left.shape[1]
    ctok = activations.shape[0]
    rtok = out_grads.shape[0]
    chunk = pick(cols, CHUNK, 128)
    nch = cols // chunk
    tile = pick(rows, TILE, 16)
    nx = nc // 2
    q = rows // nc
    dma = pltpu.SemaphoreType.DMA
    any_spec = pl.BlockSpec(memory_space=pl.ANY)
    vmem = pl.BlockSpec(memory_space=pltpu.VMEM)
    px = max(nx - 1, 1)
    pr = max(nr - 1, 1)
    pc = max(nc - 1, 1)
    left_new, left_round, descent_t, right_t, steps = pl.pallas_call(
        functools.partial(main_kernel, nr, nc, nch, chunk, tile),
        out_shape=(
            jax.ShapeDtypeStruct((rows, rank), bf16),
            jax.ShapeDtypeStruct((rows, rank), bf16),
            jax.ShapeDtypeStruct((nch, rank, chunk), bf16),
            jax.ShapeDtypeStruct((nch, rank, chunk), bf16),
            jax.ShapeDtypeStruct((2, 128), f32),
        ),
        in_specs=[any_spec] * 5,
        out_specs=(any_spec, any_spec, any_spec, any_spec, vmem),
        scratch_shapes=[
            pltpu.VMEM((rows, rank), bf16),
            pltpu.VMEM((cols, rank), bf16),
            pltpu.VMEM((rows, rank), bf16),
            pltpu.VMEM((rows, rank), bf16),
            pltpu.VMEM((nch, rows, chunk), f32),
            pltpu.VMEM((2, rows, chunk), bf16),
            pltpu.VMEM((nch, nr, rtok, chunk), bf16),
            pltpu.VMEM((nc, ctok, rows), bf16),
            pltpu.VMEM((rows, nc * ctok), bf16),
            pltpu.VMEM((nch, rank, chunk), bf16),
            pltpu.VMEM((rows, rank), f32),
            pltpu.VMEM((2, nx, q, rank), bf16),
            pltpu.VMEM((nx, q, rank), bf16),
            pltpu.VMEM((px, q, rank), bf16),
            pltpu.VMEM((px, q, rank), bf16),
            pltpu.VMEM((2, nx, q, rank), bf16),
            pltpu.VMEM((rows // tile, rank, tile), bf16),
            pltpu.VMEM((nch, rank, chunk), bf16),
            pltpu.VMEM((nch, rank, chunk), bf16),
            pltpu.VMEM((nch, rank, chunk), bf16),
            pltpu.VMEM((nch, rank, chunk), bf16),
            pltpu.VMEM((8, chunk), f32),
            pltpu.VMEM((2, nc, 8, 128), f32),
            pltpu.VMEM((2, nr, 8, 128), f32),
            dma((2,)), dma((nch,)), dma, dma((pc,)), dma((pc,)),
            dma((nch, pr)), dma((nch, pr)), dma((nch, pr)), dma((nch, pr)),
            dma((2,)), dma((px,)), dma((px,)), dma((px,)), dma((px,)), dma((2,)),
            dma((2, pc)), dma((2, pc)), dma((2, pr)), dma((2, pr)),
            dma((nch,)), dma((nch,)), dma((nch,)), dma((nch,)), dma((nch,)), dma((nch,)), dma((nch,)), dma((nch,)), dma((4,)),
        ],
        compiler_params=pltpu.CompilerParams(
            collective_id=0, has_side_effects=True, vmem_limit_bytes=66_500_000
        ),
        name="factor_steps",
    )(activations, out_grads, matrix, left, right)
    span = pick(nch, SPAN, 1)
    wide = pl.BlockSpec((rows, span * chunk), lambda i: (0, i))
    tall = pl.BlockSpec((span * chunk, rank), lambda i: (i, 0))
    flat = pl.BlockSpec((rows, rank), lambda i: (0, 0))
    turned = pl.BlockSpec((span, rank, chunk), lambda i: (i, 0, 0))
    residual, right_new = pl.pallas_call(
        functools.partial(final_kernel, span, chunk, tile),
        grid=(nch // span,),
        out_shape=(
            jax.ShapeDtypeStruct((rows, cols), bf16),
            jax.ShapeDtypeStruct((cols, rank), bf16),
        ),
        in_specs=[vmem, wide, flat, flat, flat, tall, turned, turned],
        out_specs=(wide, tall),
        compiler_params=pltpu.CompilerParams(vmem_limit_bytes=66_500_000),
        name="residual",
    )(steps, matrix, left, left_round, left_new, right, right_t, descent_t)
    return (left_new, right_new, residual)


def solution(mesh):
    placed = (
        P(("grp", "col"), "row"),
        P(("grp", "row"), "col"),
        P(("grp", "row"), "col"),
        P(("grp", "row"), None),
        P(("grp", "col"), None),
    )
    return jax.shard_map(
        functools.partial(body, mesh.shape["row"], mesh.shape["col"]),
        mesh=mesh,
        in_specs=placed,
        out_specs=(P(("grp", "row"), None), P(("grp", "col"), None), P(("grp", "row"), "col")),
        check_vma=False,
    )
```
